32 devices in a mesh: lm: 8 (over z, x), kf: 4 (over y, core).
Axes of the slice: x: 2, y: 2, z: 4, core: 2. Of those that a mesh axis runs over, the one named last changes fastest.
Arguments:
- residual_rows: bfloat16 [4096, 128], P(('lm', 'kf')), may hold values from -6 to 6
- jacobian: bfloat16 [4096, 15, 128], P(('lm', 'kf')), may hold values from -1.5 to 1.5
- nullspace: bfloat16 [4096, 128, 128], P(('lm', 'kf')), may hold values from -0.5 to 0.5
- frame_ids: int32 [4096, 64], P(('lm', 'kf')), may hold values from 0 to 16383, as said below
- obs_count: int32 [4096], P(('lm', 'kf')), may hold values from 4 to 64
- damping: float32 [15, 16384], P(None, 'kf'), may hold values from 1 to 10
- jacobi_scale: float32 [15, 16384], P(None, 'kf'), may hold values from 0.02 to 0.3
Outputs:
- solution: float32 [15, 16384], P(None, 'kf')
- residual: float32 [15, 16384], P(None, 'kf')
The draws below stay inside these ranges and needn't reach their ends.
Inputs may be any that keep to these rules, and one draw needn't show every extreme that they name: `frame_ids`: within a block the keyframe ids rise strictly from slot to slot by 1 to 8. A block stored on the device with kf index w names only keyframes from 4096 * w up to but not including 4096 * (w + 2), and never one of 16384 or more.
All inputs are finite; a program needn't handle non-finite values.
Results may differ from the reference program's by a relative error of at most 0.005.
Values sent between devices are 32-bit elements; how exact they have to be, the bound alone decides.
A program may use at most 64 MiB of HBM per device.

```python
import math
import jax
import jax.numpy as jnp
from jax import lax

STATE = 15
OBS = 64
ROWS = 128
STEP_MAX = 8
KF_DEV = 4096
BLK_DEV = 128
ITERS = 2
NK = 16384
NB = 4096
N_KF = 4


def draw_frame_ids(key, part):
    key_base = jax.random.fold_in(key, 11)
    key_gaps = jax.random.fold_in(key, 12)
    blocks = jnp.arange(NB, dtype=jnp.int32)
    window = blocks // BLK_DEV % N_KF
    limit = jnp.where(window == N_KF - 1, KF_DEV - STEP_MAX * OBS, KF_DEV)
    base = jax.random.randint(key_base, (NB,), 0, limit)
    gaps = jax.random.randint(key_gaps, (NB, OBS), 1, STEP_MAX + 1)
    offsets = jnp.cumsum(gaps, axis=1) - gaps[:, :1]
    last_base = KF_DEV - 1 - offsets[:, -1]
    base = jnp.where(blocks == 0, 0, base)
    base = jnp.where(blocks == NB - 1, last_base, base)
    return (window * KF_DEV + base)[:, None] + offsets


def touch_ends(result, stream_key, least, high):
    longest = result.shape.index(max(result.shape))
    spots = []
    for shift in (0, 1):
        where = [jax.random.randint(jax.random.fold_in(stream_key, axis), (), 0, length) for axis, length in enumerate(result.shape)]
        where[longest] = (where[longest] + shift) % result.shape[longest]
        spots.append(tuple(where))
    return result.at[spots[0]].set(least).at[spots[1]].set(high)


def block_scale(key, dims, cuts, smallest, top_value):
    level = 1.0
    for axis_at, blocks in cuts:
        draws = jax.random.uniform(jax.random.fold_in(jax.random.fold_in(key, 6), axis_at), (blocks,), jnp.float32, smallest / len(cuts), top_value / len(cuts))
        level = level * jnp.repeat(jnp.exp(draws), dims[axis_at] // blocks).reshape((-1,) + (1,) * (len(dims) - 1 - axis_at))
    return level


def gaussian(own_key, extent, scale, most, cuts=(), kind=jnp.bfloat16):
    result = jax.random.normal(own_key, extent, jnp.float32) * scale
    if len(cuts) > 0:
        result = block_scale(own_key, extent, cuts, -0.22, 0.18) * result
    return jnp.clip(result, min=-most, max=most).astype(kind)


def setup_inputs(seed: int = 0) -> dict:
    splits = jax.random.split(jax.random.key(seed), 8)
    residual_rows = gaussian(splits[0], (NB, ROWS), 1.0, 6.0, ((0, 32),))
    jacobian = gaussian(splits[1], (NB, STATE, ROWS), STATE ** -0.5, 1.5, ((0, 32),))
    nullspace = gaussian(splits[2], (NB, ROWS, ROWS), ROWS ** -0.5, 0.5, ((0, 32),))
    frame_ids = draw_frame_ids(jax.random.fold_in(splits[7], 71), 0)
    obs_count = touch_ends(jax.random.randint(splits[4], (NB,), 4, OBS + 1), jax.random.fold_in(splits[4], 1), 4, OBS).astype(jnp.int32)
    damping = jnp.clip(jnp.exp(math.log(10.0) - 2.3025851 * jax.random.uniform(splits[5], (STATE, NK), jnp.float32) ** block_scale(splits[5], (STATE, NK), ((1, 4),), -0.2, 0.2)), 1.0, 10.0)
    jacobi_scale = jnp.clip(jnp.exp(math.log(0.3) - 2.7080503 * jax.random.uniform(splits[6], (STATE, NK), jnp.float32) ** block_scale(splits[6], (STATE, NK), ((1, 4),), -0.2, 0.2)), 0.02, 0.3)
    return {"residual_rows": residual_rows, "jacobian": jacobian, "nullspace": nullspace, "frame_ids": frame_ids, "obs_count": obs_count, "damping": damping, "jacobi_scale": jacobi_scale}


def row_layout(frame_ids, obs_count):
    slots = lax.broadcasted_iota(jnp.int32, frame_ids.shape, 1)
    live = (slots < obs_count[:, None]).astype(jnp.float32)
    return jnp.repeat(frame_ids, 2, axis=1), jnp.repeat(live, 2, axis=1)


def project(lifted, nullspace, live):
    lifted_half = (lifted * live).astype(jnp.bfloat16).astype(jnp.float32)
    factor = nullspace.astype(jnp.float32)
    inner = jnp.einsum('brk,br->bk', factor, lifted_half).astype(jnp.bfloat16).astype(jnp.float32)
    spread = jnp.einsum('brk,bk->br', factor, inner)
    return spread * live


def accumulate(field, use_field, residual_rows, jacobian, nullspace, frame_ids, obs_count):
    groups = NB // BLK_DEV

    def split(arr):
        return arr.reshape((groups, BLK_DEV) + arr.shape[1:])

    def one_group(total, pieces):
        rows_res, jac_part, null_part, ids_part, count_part = pieces
        row_ids, live = row_layout(ids_part, count_part)
        if use_field:
            gathered = jnp.take(field, row_ids, axis=1)
            lifted = jnp.sum(jac_part.astype(jnp.float32) * jnp.moveaxis(gathered, 0, 1), axis=1)
        else:
            lifted = rows_res.astype(jnp.float32)
        spread = project(lifted, null_part, live)
        terms = jac_part.astype(jnp.float32) * spread[:, None, :]
        terms = jnp.moveaxis(terms, 1, 0).reshape(STATE, -1)
        return total.at[:, row_ids.reshape(-1)].add(terms), None

    start = jnp.zeros((STATE, NK), jnp.float32)
    pieces = (split(residual_rows), split(jacobian), split(nullspace), split(frame_ids), split(obs_count))
    total, unused = lax.scan(one_group, start, pieces)
    return total


def reference(residual_rows, jacobian, nullspace, frame_ids, obs_count, damping, jacobi_scale):
    gradient = -accumulate(None, False, residual_rows, jacobian, nullspace, frame_ids, obs_count)
    residual = gradient
    solution = jnp.zeros_like(gradient)
    scaled = jacobi_scale * residual
    direction = scaled
    energy = jnp.sum(residual * scaled)
    for step_index in range(ITERS):
        applied = accumulate(direction, True, residual_rows, jacobian, nullspace, frame_ids, obs_count) + damping * direction
        step_size = energy / jnp.sum(direction * applied)
        solution = solution + step_size * direction
        residual = residual - step_size * applied
        if step_index + 1 < ITERS:
            scaled = jacobi_scale * residual
            fresh = jnp.sum(residual * scaled)
            direction = scaled + (fresh / energy) * direction
            energy = fresh
    return solution, residual
```

```python
import functools

import jax
import jax.numpy as jnp
from jax import lax
from jax.experimental import pallas as pl
from jax.experimental.pallas import tpu as pltpu
from jax.sharding import PartitionSpec as P

ITERS = 2
LANES = 128
PAD = 16
SPAN = 5
CHUNK = 16


def local_kernel(use_field, starts, field_ref, code_ref, res_ref, jac_ref, null_ref, out_ref):
    step = pl.program_id(0)

    @pl.when(step == 0)
    def _():
        out_ref[...] = jnp.zeros_like(out_ref)

    lane_iota = lax.broadcasted_iota(jnp.int32, (LANES, LANES), 0)

    def one(i):
        start = starts[step * CHUNK + i]
        code = code_ref[pl.ds(i, 1), :]
        part = code >> 7
        hot = jnp.where(lane_iota == (code & (LANES - 1)), 1.0, 0.0).astype(jnp.bfloat16)
        jac = jac_ref[i].astype(jnp.float32)
        null = null_ref[i]
        if use_field:
            window = field_ref[pl.ds(start, SPAN)].reshape(SPAN * PAD, LANES).astype(jnp.bfloat16)
            spots = jnp.dot(window, hot, preferred_element_type=jnp.float32)
            gathered = jnp.zeros((PAD, LANES), jnp.float32)
            for q in range(SPAN):
                gathered = jnp.where(part == q, spots[q * PAD:(q + 1) * PAD], gathered)
            lifted = jnp.sum(jac * gathered, axis=0, keepdims=True)
        else:
            lifted = jnp.where(code >= 0, res_ref[pl.ds(i, 1), :], 0.0)
        inner = jnp.dot(
            lifted.astype(jnp.bfloat16), null, preferred_element_type=jnp.float32
        ).astype(jnp.bfloat16)
        spread = lax.dot_general(
            inner, null, (((1,), (1,)), ((), ())), preferred_element_type=jnp.float32
        )
        terms = jac * spread
        placed = jnp.concatenate(
            [jnp.where(part == q, terms, 0.0) for q in range(SPAN)], axis=0
        ).astype(jnp.bfloat16)
        back = lax.dot_general(
            placed, hot, (((1,), (1,)), ((), ())), preferred_element_type=jnp.float32
        )
        return start, back.reshape(SPAN, PAD, LANES)

    for i in range(CHUNK):
        start, back = one(i)
        out_ref[pl.ds(start, SPAN)] += back


def local_terms(use_field, starts, field, code, res, jac, null):
    blocks = null.shape[0]
    groups = field.shape[0]
    return pl.pallas_call(
        functools.partial(local_kernel, use_field),
        grid_spec=pltpu.PrefetchScalarGridSpec(
            num_scalar_prefetch=1,
            grid=(blocks // CHUNK,),
            in_specs=[
                pl.BlockSpec(field.shape, lambda b, s: (0, 0, 0)),
                pl.BlockSpec((CHUNK, LANES), lambda b, s: (b, 0)),
                pl.BlockSpec((CHUNK, LANES), lambda b, s: (b, 0)),
                pl.BlockSpec((CHUNK, PAD, LANES), lambda b, s: (b, 0, 0)),
                pl.BlockSpec((CHUNK, LANES, LANES), lambda b, s: (b, 0, 0)),
            ],
            out_specs=pl.BlockSpec((groups, PAD, LANES), lambda b, s: (0, 0, 0)),
        ),
        out_shape=jax.ShapeDtypeStruct((groups, PAD, LANES), jnp.float32),
        name="local_field" if use_field else "local_gradient",
    )(starts, field, code, res, jac, null)


def passed_along(array, axis, by):
    length = lax.axis_size(axis)
    pairs = [(i, i + by) for i in range(length) if 0 <= i + by < length]
    return lax.ppermute(array, axis, pairs)


def to_groups(array):
    state, frames = array.shape
    padded = jnp.pad(array, ((0, PAD - state), (0, 0)))
    return jnp.moveaxis(padded.reshape(PAD, frames // LANES, LANES), 1, 0)


def from_groups(array, state):
    return jnp.moveaxis(array, 0, 1).reshape(PAD, -1)[:state]


def prepare(frame_ids, obs_count, first_frame, groups):
    rel = frame_ids - first_frame
    starts = jnp.minimum(rel[:, 0] // LANES, groups - SPAN)
    slots = lax.broadcasted_iota(jnp.int32, rel.shape, 1)
    off = jnp.where(slots < obs_count[:, None], rel - starts[:, None] * LANES, -1)
    twice = (
        lax.broadcasted_iota(jnp.int32, (rel.shape[1], 2 * rel.shape[1]), 0)
        == lax.broadcasted_iota(jnp.int32, (rel.shape[1], 2 * rel.shape[1]), 1) // 2
    ).astype(jnp.float32)
    code = jnp.dot(off.astype(jnp.float32), twice, precision=lax.Precision.HIGHEST)
    return starts, jnp.round(code).astype(jnp.int32)


def shards(residual_rows, jacobian, nullspace, frame_ids, obs_count, damping, jacobi_scale):
    state, frames = damping.shape
    own = frames // LANES
    starts, code = prepare(frame_ids, obs_count, lax.axis_index("kf") * frames, 2 * own)
    jac = jnp.pad(jacobian, ((0, 0), (0, PAD - state), (0, 0)))
    res = residual_rows.astype(jnp.float32)
    damp, scale = to_groups(damping), to_groups(jacobi_scale)

    def product(field):
        if field is None:
            pair = jnp.zeros((2 * own, PAD, LANES), jnp.float32)
        else:
            pair = jnp.concatenate([field, passed_along(field, "kf", -1)], axis=0)
        total = local_terms(field is not None, starts, pair, code, res, jac, nullspace)
        return lax.psum(total[:own] + passed_along(total[own:], "kf", 1), "lm")

    def inner_window(left, right):
        return lax.psum(jnp.sum(left * right), "kf")

    residual = -product(None)
    direction = scale * residual
    energy = inner_window(residual, direction)
    answer = jnp.zeros_like(residual)
    for step_index in range(ITERS):
        applied = product(direction) + damp * direction
        step_size = energy / inner_window(direction, applied)
        answer = answer + step_size * direction
        residual = residual - step_size * applied
        if step_index + 1 < ITERS:
            scaled = scale * residual
            fresh = inner_window(residual, scaled)
            direction = scaled + fresh / energy * direction
            energy = fresh
    return (from_groups(answer, state), from_groups(residual, state))


def solution(mesh):
    placed = (
        P(("lm", "kf"), None),
        P(("lm", "kf"), None, None),
        P(("lm", "kf"), None, None),
        P(("lm", "kf"), None),
        P(("lm", "kf")),
        P(None, "kf"),
        P(None, "kf"),
    )
    return jax.shard_map(
        shards,
        mesh=mesh,
        in_specs=placed,
        out_specs=(P(None, "kf"), P(None, "kf")),
        check_vma=False,
    )
```

```python
import functools

import jax
import jax.numpy as jnp
from jax import lax
from jax.experimental import pallas as pl
from jax.experimental.pallas import tpu as pltpu
from jax.sharding import PartitionSpec as P

ITERS = 2
LANES = 128
PAD = 16
SPAN = 5
CHUNK = 16


def local_kernel(use_field, starts, field_ref, code_ref, res_ref, jac_ref, null_ref, out_ref):
    step = pl.program_id(0)

    @pl.when(step == 0)
    def _():
        out_ref[...] = jnp.zeros_like(out_ref)

    lane_iota = lax.broadcasted_iota(jnp.int32, (LANES, LANES), 0)

    def one(i):
        start = starts[step * CHUNK + i]
        code = code_ref[pl.ds(i, 1), :]
        part = code >> 7
        hot = jnp.where(lane_iota == (code & (LANES - 1)), 1.0, 0.0).astype(jnp.bfloat16)
        jac = jac_ref[i].astype(jnp.float32)
        null = null_ref[i]
        if use_field:
            window = field_ref[pl.ds(start, SPAN)].reshape(SPAN * PAD, LANES).astype(jnp.bfloat16)
            spots = jnp.dot(window, hot, preferred_element_type=jnp.float32)
            gathered = jnp.zeros((PAD, LANES), jnp.float32)
            for q in range(SPAN):
                gathered = jnp.where(part == q, spots[q * PAD:(q + 1) * PAD], gathered)
            lifted = jnp.sum(jac * gathered, axis=0, keepdims=True)
        else:
            lifted = jnp.where(code >= 0, res_ref[pl.ds(i, 1), :], 0.0)
        inner = jnp.dot(
            lifted.astype(jnp.bfloat16), null, preferred_element_type=jnp.float32
        ).astype(jnp.bfloat16)
        spread = lax.dot_general(
            inner, null, (((1,), (1,)), ((), ())), preferred_element_type=jnp.float32
        )
        terms = jac * spread
        placed = jnp.concatenate(
            [jnp.where(part == q, terms, 0.0) for q in range(SPAN)], axis=0
        ).astype(jnp.bfloat16)
        back = lax.dot_general(
            placed, hot, (((1,), (1,)), ((), ())), preferred_element_type=jnp.float32
        )
        return start, back.reshape(SPAN, PAD, LANES)

    for i in range(CHUNK):
        start, back = one(i)
        out_ref[pl.ds(start, SPAN)] += back


def local_terms(use_field, starts, field, code, res, jac, null):
    blocks = null.shape[0]
    groups = field.shape[0]
    return pl.pallas_call(
        functools.partial(local_kernel, use_field),
        grid_spec=pltpu.PrefetchScalarGridSpec(
            num_scalar_prefetch=1,
            grid=(blocks // CHUNK,),
            in_specs=[
                pl.BlockSpec(field.shape, lambda b, s: (0, 0, 0)),
                pl.BlockSpec((CHUNK, LANES), lambda b, s: (b, 0)),
                pl.BlockSpec((CHUNK, LANES), lambda b, s: (b, 0)),
                pl.BlockSpec((CHUNK, PAD, LANES), lambda b, s: (b, 0, 0)),
                pl.BlockSpec((CHUNK, LANES, LANES), lambda b, s: (b, 0, 0)),
            ],
            out_specs=pl.BlockSpec((groups, PAD, LANES), lambda b, s: (0, 0, 0)),
        ),
        out_shape=jax.ShapeDtypeStruct((groups, PAD, LANES), jnp.float32),
        name="local_field" if use_field else "local_gradient",
    )(starts, field, code, res, jac, null)


def passed_along(array, axis, by):
    length = lax.axis_size(axis)
    pairs = [(i, i + by) for i in range(length) if 0 <= i + by < length]
    return lax.ppermute(array, axis, pairs)


def remote(src, dst, send, recv, axis, index):
    return pltpu.make_async_remote_copy(
        src_ref=src, dst_ref=dst, send_sem=send, recv_sem=recv,
        device_id={axis: index}, device_id_type=pl.DeviceIdType.MESH,
    )


def greet(n, m):
    i, w = lax.axis_index("lm"), lax.axis_index("kf")
    barrier = pltpu.get_barrier_semaphore()
    for k in range(1, n):
        pl.semaphore_signal(
            barrier, inc=1, device_id={"lm": lax.rem(i + k, n)}, device_id_type=pl.DeviceIdType.MESH
        )
    for k in range(1, m):
        pl.semaphore_signal(
            barrier, inc=1, device_id={"kf": lax.rem(w + k, m)}, device_id_type=pl.DeviceIdType.MESH
        )
    pl.semaphore_wait(barrier, n - 1 + m - 1)


def reduce_spread(n, m, pair, h, full, bufs, sems):
    fold, acc, rs = bufs
    fold_s, fold_r, rs_s, rs_r, ag_s, ag_r, fw_s, fw_r = sems
    own = acc.shape[0]
    sh = own // n
    i, w = lax.axis_index("lm"), lax.axis_index("kf")
    later, former = lax.rem(w + 1, m), lax.rem(w + m - 1, m)

    def at(ref, j, base=0):
        return ref.at[pl.ds(base + j * sh, sh)]

    order = [lax.rem(i + k, n) for k in range(1, n)] + [i]
    others = order[:-1]
    folds = [remote(at(h, j, own), at(fold, j), fold_s.at[k], fold_r.at[k], "kf", later) for k, j in enumerate(order)]

    @pl.when(w < m - 1)
    def _():
        for copy in folds:
            copy.start()

    scatters = [remote(at(acc, j), rs.at[i], rs_s.at[k], rs_r.at[i], "lm", j) for k, j in enumerate(others)]
    for k, j in enumerate(order):
        spot = pl.ds(j * sh, sh)

        @pl.when(w > 0)
        def _():
            folds[k].wait_recv()
            acc[spot] = h[spot] + fold[spot]

        @pl.when(w == 0)
        def _():
            acc[spot] = h[spot]

        if k < n - 1:
            scatters[k].start()
    total = acc[pl.ds(i * sh, sh)]
    arrive = [lax.rem(i + n - k, n) for k in range(1, n)]
    for j in arrive:
        remote(at(acc, j), rs.at[j], rs_s.at[0], rs_r.at[j], "lm", j).wait_recv()
        total = total + rs[j]
    full[pl.ds(i * sh, sh)] = total
    gathers = [remote(at(full, i), at(full, i), ag_s.at[k], ag_r.at[i], "lm", j) for k, j in enumerate(others)]
    for copy in gathers:
        copy.start()
    forwards = []
    for k, j in enumerate([i] + arrive):
        if k > 0:
            remote(at(full, j), at(full, j), ag_s.at[0], ag_r.at[j], "lm", j).wait_recv()
        if pair:
            copy = remote(at(full, j), at(full, j, own), fw_s.at[k], fw_r.at[k], "kf", former)
            forwards.append(copy)

            @pl.when(w > 0)
            def _():
                copy.start()

    def finish_pair():
        @pl.when(w < m - 1)
        def _():
            for copy in forwards:
                copy.wait_recv()

        @pl.when(w == m - 1)
        def _():
            full[pl.ds(own, own)] = jnp.zeros((own,) + full.shape[1:], jnp.float32)

    def finish_sends():
        @pl.when(w < m - 1)
        def _():
            for copy in folds:
                copy.wait_send()

        for copy in scatters + gathers:
            copy.wait_send()
        if pair:

            @pl.when(w > 0)
            def _():
                for copy in forwards:
                    copy.wait_send()

    return finish_pair, finish_sends


def over_windows(m, value, slots, send, recv):
    w = lax.axis_index("kf")
    slots[w] = jnp.sum(value, axis=0)
    copies = []
    for k in range(1, m):
        copy = remote(slots.at[w], slots.at[w], send.at[k], recv.at[w], "kf", lax.rem(w + k, m))
        copy.start()
        copies.append(copy)
    for k in range(1, m):
        j = lax.rem(w + k, m)
        remote(slots.at[j], slots.at[j], send.at[0], recv.at[j], "kf", j).wait_recv()
    total = slots[0]
    for j in range(1, m):
        total = total + slots[j]

    def finish():
        for copy in copies:
            copy.wait_send()

    return jnp.sum(jnp.sum(total, axis=0, keepdims=True), axis=1, keepdims=True), finish


def first_phase(n, m, h, scale, res_out, dir_out, energy_out, full, fold, acc, rs, slots, *sems):
    own = acc.shape[0]
    greet(n, m)
    finish_pair, finish_sends = reduce_spread(n, m, True, h, full, (fold, acc, rs), sems[:8])
    grad = full[pl.ds(0, own)]
    energy, finish = over_windows(m, grad * grad * scale[pl.ds(0, own)], slots.at[0], sems[8].at[0], sems[9].at[0])
    energy_out[...] = jnp.broadcast_to(energy, energy_out.shape)
    finish_pair()
    res_out[...] = -full[...]
    dir_out[...] = -full[...] * scale[...]
    finish()
    finish_sends()


def middle_phase(n, m, h, res, direction, scale, damp, energy_in, answer_in, res_out, dir_out, energy_out, answer_out, full, fold, acc, rs, slots, *sems):
    own = acc.shape[0]
    here = pl.ds(0, own)
    greet(n, m)
    finish_pair, finish_sends = reduce_spread(n, m, True, h, full, (fold, acc, rs), sems[:8])
    energy = energy_in[pl.ds(0, 1), pl.ds(0, 1)]
    applied = full[here] + damp[here] * direction[here]
    curve, finish_a = over_windows(m, direction[here] * applied, slots.at[0], sems[8].at[0], sems[9].at[0])
    step = energy / curve
    after = res[here] - step * applied
    fresh, finish_b = over_windows(m, after * after * scale[here], slots.at[1], sems[8].at[1], sems[9].at[1])
    answer_out[...] = answer_in[...] + step * direction[here]
    energy_out[...] = jnp.broadcast_to(fresh, energy_out.shape)
    finish_pair()
    after = res[...] - step * (full[...] + damp[...] * direction[...])
    res_out[...] = after
    dir_out[...] = scale[...] * after + fresh / energy * direction[...]
    finish_a()
    finish_b()
    finish_sends()


def last_phase(n, m, h, res, direction, damp, energy_in, answer_in, res_out, answer_out, full, fold, acc, rs, slots, *sems):
    own = acc.shape[0]
    here = pl.ds(0, own)
    greet(n, m)
    _, finish_sends = reduce_spread(n, m, False, h, full, (fold, acc, rs), sems[:8])
    applied = full[here] + damp[here] * direction[here]
    curve, finish = over_windows(m, direction[here] * applied, slots.at[0], sems[8].at[0], sems[9].at[0])
    step = energy_in[pl.ds(0, 1), pl.ds(0, 1)] / curve
    answer_out[...] = answer_in[...] + step * direction[here]
    res_out[...] = res[here] - step * applied
    finish()
    finish_sends()


def phase(kernel, number, n, m, outs, *operands):
    pair = operands[0].shape
    own = pair[0] // 2
    tile = pair[1:]
    vmem = pl.BlockSpec(memory_space=pltpu.VMEM)
    dma = pltpu.SemaphoreType.DMA
    return pl.pallas_call(
        functools.partial(kernel, n, m),
        in_specs=[vmem] * len(operands),
        out_specs=[vmem] * len(outs),
        out_shape=[jax.ShapeDtypeStruct(shape, jnp.float32) for shape in outs],
        scratch_shapes=[
            pltpu.VMEM(pair, jnp.float32),
            pltpu.VMEM((own,) + tile, jnp.float32),
            pltpu.VMEM((own,) + tile, jnp.float32),
            pltpu.VMEM((n, own // n) + tile, jnp.float32),
            pltpu.VMEM((2, m) + tile, jnp.float32),
        ]
        + [dma((n,))] * 8
        + [dma((2, m))] * 2,
        compiler_params=pltpu.CompilerParams(collective_id=number, has_side_effects=True),
        name=kernel.__name__,
    )(*operands)


def to_groups(array):
    state, frames = array.shape
    padded = jnp.pad(array, ((0, PAD - state), (0, 0)))
    return jnp.moveaxis(padded.reshape(PAD, frames // LANES, LANES), 1, 0)


def from_groups(array, state):
    return jnp.moveaxis(array, 0, 1).reshape(PAD, -1)[:state]


def prepare(frame_ids, obs_count, first_frame, groups):
    rel = frame_ids - first_frame
    starts = jnp.minimum(rel[:, 0] // LANES, groups - SPAN)
    slots = lax.broadcasted_iota(jnp.int32, rel.shape, 1)
    off = jnp.where(slots < obs_count[:, None], rel - starts[:, None] * LANES, -1)
    twice = (
        lax.broadcasted_iota(jnp.int32, (rel.shape[1], 2 * rel.shape[1]), 0)
        == lax.broadcasted_iota(jnp.int32, (rel.shape[1], 2 * rel.shape[1]), 1) // 2
    ).astype(jnp.float32)
    code = jnp.dot(off.astype(jnp.float32), twice, precision=lax.Precision.HIGHEST)
    return starts, jnp.round(code).astype(jnp.int32)


def shards(residual_rows, jacobian, nullspace, frame_ids, obs_count, damping, jacobi_scale):
    state, frames = damping.shape
    own = frames // LANES
    starts, code = prepare(frame_ids, obs_count, lax.axis_index("kf") * frames, 2 * own)
    jac = jnp.pad(jacobian, ((0, 0), (0, PAD - state), (0, 0)))
    res = residual_rows.astype(jnp.float32)
    n, m = lax.axis_size("lm"), lax.axis_size("kf")
    window = jnp.concatenate([to_groups(damping), to_groups(jacobi_scale)], axis=1)
    window = jnp.concatenate([window, passed_along(window, "kf", -1)], axis=0)
    damp, scale = window[:, :PAD], window[:, PAD:]
    pair, one, tile = (2 * own, PAD, LANES), (own, PAD, LANES), (8, LANES)

    def product(field):
        used = field is not None
        held = field if used else jnp.zeros(pair, jnp.float32)
        return local_terms(used, starts, held, code, res, jac, nullspace)

    residual, direction, energy = phase(first_phase, 0, n, m, (pair, pair, tile), product(None), scale)
    answer = jnp.zeros(one, jnp.float32)
    for number in range(1, ITERS):
        residual, direction, energy, answer = phase(
            middle_phase, number, n, m, (pair, pair, tile, one),
            product(direction), residual, direction, scale, damp, energy, answer,
        )
    residual, answer = phase(
        last_phase, ITERS, n, m, (one, one), product(direction), residual, direction, damp, energy, answer
    )
    return (from_groups(answer, state), from_groups(residual, state))


def solution(mesh):
    placed = (
        P(("lm", "kf"), None),
        P(("lm", "kf"), None, None),
        P(("lm", "kf"), None, None),
        P(("lm", "kf"), None),
        P(("lm", "kf")),
        P(None, "kf"),
        P(None, "kf"),
    )
    return jax.shard_map(
        shards,
        mesh=mesh,
        in_specs=placed,
        out_specs=(P(None, "kf"), P(None, "kf")),
        check_vma=False,
    )
```

```python
import functools

import jax
import jax.numpy as jnp
from jax import lax
from jax.experimental import pallas as pl
from jax.experimental.pallas import tpu as pltpu
from jax.sharding import PartitionSpec as P

ITERS = 2
LANES = 128
PAD = 16
SPAN = 5
CHUNK = 16


def local_kernel(use_field, starts, field_ref, code_ref, res_ref, jac_ref, null_ref, out_ref, hot_ref, row_ref):
    step = pl.program_id(0)

    @pl.when(step == 0)
    def _():
        out_ref[...] = jnp.zeros_like(out_ref)

    lane_iota = lax.broadcasted_iota(jnp.int32, (LANES, LANES), 0)
    codes = [code_ref[pl.ds(i, 1), :] for i in range(CHUNK)]
    begin = [starts[step * CHUNK + i] for i in range(CHUNK)]
    for i in range(CHUNK):
        hot = lane_iota == (codes[i] & (LANES - 1))
        hot_ref[i] = jnp.where(hot, 1.0, 0.0).astype(jnp.bfloat16)
    if use_field:
        for i in range(CHUNK):
            window = field_ref[pl.ds(begin[i], SPAN)].reshape(SPAN * PAD, LANES).astype(jnp.bfloat16)
            spots = jnp.dot(window, hot_ref[i], preferred_element_type=jnp.float32)
            part = codes[i] >> 7
            gathered = jnp.zeros((PAD, LANES), jnp.float32)
            for q in range(SPAN):
                gathered = jnp.where(part == q, spots[q * PAD:(q + 1) * PAD], gathered)
            jac = jac_ref[i].astype(jnp.float32)
            row_ref[pl.ds(i, 1), :] = jnp.sum(jac * gathered, axis=0, keepdims=True)
    else:
        row_ref[...] = jnp.where(code_ref[...] >= 0, res_ref[...], 0.0)
    inner = []
    for i in range(CHUNK):
        lifted = row_ref[pl.ds(i, 1), :].astype(jnp.bfloat16)
        inner.append(jnp.dot(lifted, null_ref[i], preferred_element_type=jnp.float32).astype(jnp.bfloat16))
    for i in range(CHUNK):
        row_ref[pl.ds(i, 1), :] = lax.dot_general(
            inner[i], null_ref[i], (((1,), (1,)), ((), ())), preferred_element_type=jnp.float32
        )
    back = []
    for i in range(CHUNK):
        part = codes[i] >> 7
        terms = jac_ref[i].astype(jnp.float32) * row_ref[pl.ds(i, 1), :]
        placed = jnp.concatenate(
            [jnp.where(part == q, terms, 0.0) for q in range(SPAN)], axis=0
        ).astype(jnp.bfloat16)
        back.append(lax.dot_general(
            placed, hot_ref[i], (((1,), (1,)), ((), ())), preferred_element_type=jnp.float32
        ).reshape(SPAN, PAD, LANES))
    for i in range(CHUNK):
        out_ref[pl.ds(begin[i], SPAN)] += back[i]


def local_terms(use_field, starts, field, code, res, jac, null):
    blocks = null.shape[0]
    groups = field.shape[0]
    return pl.pallas_call(
        functools.partial(local_kernel, use_field),
        grid_spec=pltpu.PrefetchScalarGridSpec(
            num_scalar_prefetch=1,
            grid=(blocks // CHUNK,),
            in_specs=[
                pl.BlockSpec(field.shape, lambda b, s: (0, 0, 0)),
                pl.BlockSpec((CHUNK, LANES), lambda b, s: (b, 0)),
                pl.BlockSpec((CHUNK, LANES), lambda b, s: (b, 0)),
                pl.BlockSpec((CHUNK, PAD, LANES), lambda b, s: (b, 0, 0)),
                pl.BlockSpec((CHUNK, LANES, LANES), lambda b, s: (b, 0, 0)),
            ],
            out_specs=pl.BlockSpec((groups, PAD, LANES), lambda b, s: (0, 0, 0)),
            scratch_shapes=[
                pltpu.VMEM((CHUNK, LANES, LANES), jnp.bfloat16),
                pltpu.VMEM((CHUNK, LANES), jnp.float32),
            ],
        ),
        out_shape=jax.ShapeDtypeStruct((groups, PAD, LANES), jnp.float32),
        name="local_field" if use_field else "local_gradient",
    )(starts, field, code, res, jac, null)


def passed_along(array, axis, by):
    length = lax.axis_size(axis)
    pairs = [(i, i + by) for i in range(length) if 0 <= i + by < length]
    return lax.ppermute(array, axis, pairs)


def remote(src, dst, send, recv, axis, index):
    return pltpu.make_async_remote_copy(
        src_ref=src, dst_ref=dst, send_sem=send, recv_sem=recv,
        device_id={axis: index}, device_id_type=pl.DeviceIdType.MESH,
    )


def greet(n, m):
    i, w = lax.axis_index("lm"), lax.axis_index("kf")
    barrier = pltpu.get_barrier_semaphore()
    for k in range(1, n):
        pl.semaphore_signal(
            barrier, inc=1, device_id={"lm": lax.rem(i + k, n)}, device_id_type=pl.DeviceIdType.MESH
        )
    for k in range(1, m):
        pl.semaphore_signal(
            barrier, inc=1, device_id={"kf": lax.rem(w + k, m)}, device_id_type=pl.DeviceIdType.MESH
        )
    pl.semaphore_wait(barrier, n - 1 + m - 1)


def reduce_spread(n, m, pair, h, full, bufs, sems):
    fold, acc, rs = bufs
    fold_s, fold_r, rs_s, rs_r, ag_s, ag_r, fw_s, fw_r = sems
    own = acc.shape[0]
    sh = own // n
    i, w = lax.axis_index("lm"), lax.axis_index("kf")
    later, former = lax.rem(w + 1, m), lax.rem(w + m - 1, m)

    def at(ref, j, base=0):
        return ref.at[pl.ds(base + j * sh, sh)]

    order = [lax.rem(i + k, n) for k in range(1, n)] + [i]
    others = order[:-1]
    folds = [remote(at(h, j, own), at(fold, j), fold_s.at[k], fold_r.at[k], "kf", later) for k, j in enumerate(order)]

    @pl.when(w < m - 1)
    def _():
        for copy in folds:
            copy.start()

    scatters = [remote(at(acc, j), rs.at[i], rs_s.at[k], rs_r.at[i], "lm", j) for k, j in enumerate(others)]
    for k, j in enumerate(order):
        spot = pl.ds(j * sh, sh)

        @pl.when(w > 0)
        def _():
            folds[k].wait_recv()
            acc[spot] = h[spot] + fold[spot]

        @pl.when(w == 0)
        def _():
            acc[spot] = h[spot]

        if k < n - 1:
            scatters[k].start()
    total = acc[pl.ds(i * sh, sh)]
    arrive = [lax.rem(i + n - k, n) for k in range(1, n)]
    for j in arrive:
        remote(at(acc, j), rs.at[j], rs_s.at[0], rs_r.at[j], "lm", j).wait_recv()
        total = total + rs[j]
    full[pl.ds(i * sh, sh)] = total
    gathers = [remote(at(full, i), at(full, i), ag_s.at[k], ag_r.at[i], "lm", j) for k, j in enumerate(others)]
    for copy in gathers:
        copy.start()
    forwards = []
    for k, j in enumerate([i] + arrive):
        if k > 0:
            remote(at(full, j), at(full, j), ag_s.at[0], ag_r.at[j], "lm", j).wait_recv()
        if pair:
            copy = remote(at(full, j), at(full, j, own), fw_s.at[k], fw_r.at[k], "kf", former)
            forwards.append(copy)

            @pl.when(w > 0)
            def _():
                copy.start()

    def finish_pair():
        @pl.when(w < m - 1)
        def _():
            for copy in forwards:
                copy.wait_recv()

        @pl.when(w == m - 1)
        def _():
            full[pl.ds(own, own)] = jnp.zeros((own,) + full.shape[1:], jnp.float32)

    def finish_sends():
        @pl.when(w < m - 1)
        def _():
            for copy in folds:
                copy.wait_send()

        for copy in scatters + gathers:
            copy.wait_send()
        if pair:

            @pl.when(w > 0)
            def _():
                for copy in forwards:
                    copy.wait_send()

    return finish_pair, finish_sends


def over_windows(m, value, slots, send, recv):
    w = lax.axis_index("kf")
    slots[w] = jnp.sum(value, axis=0)
    copies = []
    for k in range(1, m):
        copy = remote(slots.at[w], slots.at[w], send.at[k], recv.at[w], "kf", lax.rem(w + k, m))
        copy.start()
        copies.append(copy)
    for k in range(1, m):
        j = lax.rem(w + k, m)
        remote(slots.at[j], slots.at[j], send.at[0], recv.at[j], "kf", j).wait_recv()
    total = slots[0]
    for j in range(1, m):
        total = total + slots[j]

    def finish():
        for copy in copies:
            copy.wait_send()

    return jnp.sum(jnp.sum(total, axis=0, keepdims=True), axis=1, keepdims=True), finish


def first_phase(n, m, h, scale, res_out, dir_out, energy_out, full, fold, acc, rs, slots, *sems):
    own = acc.shape[0]
    greet(n, m)
    finish_pair, finish_sends = reduce_spread(n, m, True, h, full, (fold, acc, rs), sems[:8])
    grad = full[pl.ds(0, own)]
    energy, finish = over_windows(m, grad * grad * scale[pl.ds(0, own)], slots.at[0], sems[8].at[0], sems[9].at[0])
    energy_out[...] = jnp.broadcast_to(energy, energy_out.shape)
    finish_pair()
    res_out[...] = -full[...]
    dir_out[...] = -full[...] * scale[...]
    finish()
    finish_sends()


def middle_phase(n, m, h, res, direction, scale, damp, energy_in, answer_in, res_out, dir_out, energy_out, answer_out, full, fold, acc, rs, slots, *sems):
    own = acc.shape[0]
    here = pl.ds(0, own)
    greet(n, m)
    finish_pair, finish_sends = reduce_spread(n, m, True, h, full, (fold, acc, rs), sems[:8])
    energy = energy_in[pl.ds(0, 1), pl.ds(0, 1)]
    applied = full[here] + damp[here] * direction[here]
    curve, finish_a = over_windows(m, direction[here] * applied, slots.at[0], sems[8].at[0], sems[9].at[0])
    step = energy / curve
    after = res[here] - step * applied
    fresh, finish_b = over_windows(m, after * after * scale[here], slots.at[1], sems[8].at[1], sems[9].at[1])
    answer_out[...] = answer_in[...] + step * direction[here]
    energy_out[...] = jnp.broadcast_to(fresh, energy_out.shape)
    finish_pair()
    after = res[...] - step * (full[...] + damp[...] * direction[...])
    res_out[...] = after
    dir_out[...] = scale[...] * after + fresh / energy * direction[...]
    finish_a()
    finish_b()
    finish_sends()


def last_phase(n, m, h, res, direction, damp, energy_in, answer_in, res_out, answer_out, full, fold, acc, rs, slots, *sems):
    own = acc.shape[0]
    here = pl.ds(0, own)
    greet(n, m)
    _, finish_sends = reduce_spread(n, m, False, h, full, (fold, acc, rs), sems[:8])
    applied = full[here] + damp[here] * direction[here]
    curve, finish = over_windows(m, direction[here] * applied, slots.at[0], sems[8].at[0], sems[9].at[0])
    step = energy_in[pl.ds(0, 1), pl.ds(0, 1)] / curve
    answer_out[...] = answer_in[...] + step * direction[here]
    res_out[...] = res[here] - step * applied
    finish()
    finish_sends()


def phase(kernel, number, n, m, outs, *operands):
    pair = operands[0].shape
    own = pair[0] // 2
    tile = pair[1:]
    vmem = pl.BlockSpec(memory_space=pltpu.VMEM)
    dma = pltpu.SemaphoreType.DMA
    return pl.pallas_call(
        functools.partial(kernel, n, m),
        in_specs=[vmem] * len(operands),
        out_specs=[vmem] * len(outs),
        out_shape=[jax.ShapeDtypeStruct(shape, jnp.float32) for shape in outs],
        scratch_shapes=[
            pltpu.VMEM(pair, jnp.float32),
            pltpu.VMEM((own,) + tile, jnp.float32),
            pltpu.VMEM((own,) + tile, jnp.float32),
            pltpu.VMEM((n, own // n) + tile, jnp.float32),
            pltpu.VMEM((2, m) + tile, jnp.float32),
        ]
        + [dma((n,))] * 8
        + [dma((2, m))] * 2,
        compiler_params=pltpu.CompilerParams(collective_id=number, has_side_effects=True),
        name=kernel.__name__,
    )(*operands)


def to_groups(array):
    state, frames = array.shape
    padded = jnp.pad(array, ((0, PAD - state), (0, 0)))
    return jnp.moveaxis(padded.reshape(PAD, frames // LANES, LANES), 1, 0)


def from_groups(array, state):
    return jnp.moveaxis(array, 0, 1).reshape(PAD, -1)[:state]


def prepare(frame_ids, obs_count, first_frame, groups):
    rel = frame_ids - first_frame
    starts = jnp.minimum(rel[:, 0] // LANES, groups - SPAN)
    slots = lax.broadcasted_iota(jnp.int32, rel.shape, 1)
    off = jnp.where(slots < obs_count[:, None], rel - starts[:, None] * LANES, -1)
    twice = (
        lax.broadcasted_iota(jnp.int32, (rel.shape[1], 2 * rel.shape[1]), 0)
        == lax.broadcasted_iota(jnp.int32, (rel.shape[1], 2 * rel.shape[1]), 1) // 2
    ).astype(jnp.float32)
    code = jnp.dot(off.astype(jnp.float32), twice, precision=lax.Precision.HIGHEST)
    return starts, jnp.round(code).astype(jnp.int32)


def shards(residual_rows, jacobian, nullspace, frame_ids, obs_count, damping, jacobi_scale):
    state, frames = damping.shape
    own = frames // LANES
    starts, code = prepare(frame_ids, obs_count, lax.axis_index("kf") * frames, 2 * own)
    jac = jnp.pad(jacobian, ((0, 0), (0, PAD - state), (0, 0)))
    res = residual_rows.astype(jnp.float32)
    n, m = lax.axis_size("lm"), lax.axis_size("kf")
    window = jnp.concatenate([to_groups(damping), to_groups(jacobi_scale)], axis=1)
    window = jnp.concatenate([window, passed_along(window, "kf", -1)], axis=0)
    damp, scale = window[:, :PAD], window[:, PAD:]
    pair, one, tile = (2 * own, PAD, LANES), (own, PAD, LANES), (8, LANES)

    def product(field):
        used = field is not None
        held = field if used else jnp.zeros(pair, jnp.float32)
        return local_terms(used, starts, held, code, res, jac, nullspace)

    residual, direction, energy = phase(first_phase, 0, n, m, (pair, pair, tile), product(None), scale)
    answer = jnp.zeros(one, jnp.float32)
    for number in range(1, ITERS):
        residual, direction, energy, answer = phase(
            middle_phase, number, n, m, (pair, pair, tile, one),
            product(direction), residual, direction, scale, damp, energy, answer,
        )
    residual, answer = phase(
        last_phase, ITERS, n, m, (one, one), product(direction), residual, direction, damp, energy, answer
    )
    return (from_groups(answer, state), from_groups(residual, state))


def solution(mesh):
    placed = (
        P(("lm", "kf"), None),
        P(("lm", "kf"), None, None),
        P(("lm", "kf"), None, None),
        P(("lm", "kf"), None),
        P(("lm", "kf")),
        P(None, "kf"),
        P(None, "kf"),
    )
    return jax.shard_map(
        shards,
        mesh=mesh,
        in_specs=placed,
        out_specs=(P(None, "kf"), P(None, "kf")),
        check_vma=False,
    )
```

```python
import functools

import jax
import jax.numpy as jnp
from jax import lax
from jax.experimental import pallas as pl
from jax.experimental.pallas import tpu as pltpu
from jax.sharding import PartitionSpec as P

ITERS = 2
LANES = 128
PAD = 16
SPAN = 5
CHUNK = 16


def local_kernel(use_field, starts, field_ref, code_ref, jac_ref, null_ref, out_ref, hot_ref, row_ref):
    step = pl.program_id(0)

    @pl.when(step == 0)
    def _():
        out_ref[...] = jnp.zeros_like(out_ref)

    lane_iota = lax.broadcasted_iota(jnp.int32, (LANES, LANES), 0)
    codes = [code_ref[pl.ds(i, 1), :] for i in range(CHUNK)]
    begin = [starts[step * CHUNK + i] for i in range(CHUNK)]
    for i in range(CHUNK):
        hot = lane_iota == (codes[i] & (LANES - 1))
        hot_ref[i] = jnp.where(hot, 1.0, 0.0).astype(jnp.bfloat16)
    if use_field:
        for i in range(CHUNK):
            window = field_ref[pl.ds(begin[i], SPAN)].reshape(SPAN * PAD, LANES).astype(jnp.bfloat16)
            spots = jnp.dot(window, hot_ref[i], preferred_element_type=jnp.float32)
            part = codes[i] >> 7
            gathered = jnp.zeros((PAD, LANES), jnp.float32)
            for q in range(SPAN):
                gathered = jnp.where(part == q, spots[q * PAD:(q + 1) * PAD], gathered)
            jac = jac_ref[i].astype(jnp.float32)
            row_ref[pl.ds(i, 1), :] = jnp.sum(jac * gathered, axis=0, keepdims=True)
    else:
        row_ref[...] = jnp.where(code_ref[...] >= 0, field_ref[...].astype(jnp.float32), 0.0)
    inner = []
    for i in range(CHUNK):
        lifted = row_ref[pl.ds(i, 1), :].astype(jnp.bfloat16)
        inner.append(jnp.dot(lifted, null_ref[i], preferred_element_type=jnp.float32).astype(jnp.bfloat16))
    for i in range(CHUNK):
        row_ref[pl.ds(i, 1), :] = lax.dot_general(
            inner[i], null_ref[i], (((1,), (1,)), ((), ())), preferred_element_type=jnp.float32
        )
    back = []
    for i in range(CHUNK):
        part = codes[i] >> 7
        terms = jac_ref[i].astype(jnp.float32) * row_ref[pl.ds(i, 1), :]
        placed = jnp.concatenate(
            [jnp.where(part == q, terms, 0.0) for q in range(SPAN)], axis=0
        ).astype(jnp.bfloat16)
        back.append(lax.dot_general(
            placed, hot_ref[i], (((1,), (1,)), ((), ())), preferred_element_type=jnp.float32
        ).reshape(SPAN, PAD, LANES))
    for i in range(CHUNK):
        out_ref[pl.ds(begin[i], SPAN)] += back[i]


def local_terms(use_field, starts, field, code, jac, null, groups):
    blocks = null.shape[0]
    if use_field:
        source = pl.BlockSpec(field.shape, lambda b, s: (0, 0, 0))
    else:
        source = pl.BlockSpec((CHUNK, LANES), lambda b, s: (b, 0))
    return pl.pallas_call(
        functools.partial(local_kernel, use_field),
        grid_spec=pltpu.PrefetchScalarGridSpec(
            num_scalar_prefetch=1,
            grid=(blocks // CHUNK,),
            in_specs=[
                source,
                pl.BlockSpec((CHUNK, LANES), lambda b, s: (b, 0)),
                pl.BlockSpec((CHUNK, PAD, LANES), lambda b, s: (b, 0, 0)),
                pl.BlockSpec((CHUNK, LANES, LANES), lambda b, s: (b, 0, 0)),
            ],
            out_specs=pl.BlockSpec((groups, PAD, LANES), lambda b, s: (0, 0, 0)),
            scratch_shapes=[
                pltpu.VMEM((CHUNK, LANES, LANES), jnp.bfloat16),
                pltpu.VMEM((CHUNK, LANES), jnp.float32),
            ],
        ),
        out_shape=jax.ShapeDtypeStruct((groups, PAD, LANES), jnp.float32),
        name="local_field" if use_field else "local_gradient",
    )(starts, field, code, jac, null)


def remote(src, dst, send, recv, axis, index):
    return pltpu.make_async_remote_copy(
        src_ref=src, dst_ref=dst, send_sem=send, recv_sem=recv,
        device_id={axis: index}, device_id_type=pl.DeviceIdType.MESH,
    )


def greet(n, m):
    i, w = lax.axis_index("lm"), lax.axis_index("kf")
    barrier = pltpu.get_barrier_semaphore()
    peers = [("lm", i + 1 - 2 * lax.rem(i, 2))]
    peers += [("lm", lax.rem(i + 2 * k, n)) for k in range(1, n // 2)]
    peers += [("kf", lax.rem(w + k, m)) for k in range(1, m)]
    for axis, index in peers:
        pl.semaphore_signal(barrier, inc=1, device_id={axis: index}, device_id_type=pl.DeviceIdType.MESH)
    pl.semaphore_wait(barrier, len(peers))


def reduce_spread(n, m, pair, h, full, bufs, sems):
    fold, acc, twin, rs = bufs
    fold_s, fold_r, tw_s, tw_r, rs_s, rs_r, ag_s, xs_s, ag_r, fw_s, fw_r = sems
    own = acc.shape[0]
    sh = own // n
    hi = n // 2
    i, w = lax.axis_index("lm"), lax.axis_index("kf")
    z, x = i // 2, lax.rem(i, 2)
    partner = i + 1 - 2 * x
    later, former = lax.rem(w + 1, m), lax.rem(w + m - 1, m)

    def at(ref, j, base=0):
        return ref.at[pl.ds(base + j * sh, sh)]

    levels = [lax.rem(z + k, hi) for k in range(1, hi)] + [z]
    near = [2 * level + x for level in levels]
    far = [2 * level + 1 - x for level in levels]
    order = [j for k in range(hi) for j in (far[k], near[k])]
    folds = [remote(at(h, j, own), at(fold, j), fold_s.at[k], fold_r.at[k], "kf", later) for k, j in enumerate(order)]

    @pl.when(w < m - 1)
    def _():
        for copy in folds:
            copy.start()

    twins = [remote(at(acc, far[k]), twin.at[k], tw_s.at[k], tw_r.at[k], "lm", partner) for k in range(hi)]
    scatters = [remote(at(acc, near[k]), rs.at[z], rs_s.at[k], rs_r.at[z], "lm", near[k]) for k in range(hi - 1)]

    def take(k):
        spot = pl.ds(order[k] * sh, sh)

        @pl.when(w > 0)
        def _():
            folds[k].wait_recv()
            acc[spot] = h[spot] + fold[spot]

        @pl.when(w == 0)
        def _():
            acc[spot] = h[spot]

    def join(k):
        twins[k].wait_recv()
        spot = pl.ds(near[k] * sh, sh)
        acc[spot] = acc[spot] + twin[k]
        if k < hi - 1:
            scatters[k].start()

    for k in range(hi):
        take(2 * k)
        twins[k].start()
        take(2 * k + 1)
        if k > 0:
            join(k - 1)
    join(hi - 1)
    total = acc[pl.ds(i * sh, sh)]
    arrive = [lax.rem(z + hi - k, hi) for k in range(1, hi)]
    for level in arrive:
        j = 2 * level + x
        remote(at(acc, j), rs.at[level], rs_s.at[0], rs_r.at[level], "lm", j).wait_recv()
        total = total + rs[level]
    full[pl.ds(i * sh, sh)] = total
    gathers = [remote(at(full, i), at(full, i), ag_s.at[k], ag_r.at[i], "lm", near[k]) for k in range(hi - 1)]
    for copy in gathers:
        copy.start()
    crosses, forwards = [], []

    def pass_on(j, cross):
        if cross:
            copy = remote(at(full, j), at(full, j), xs_s.at[len(crosses)], ag_r.at[j], "lm", partner)
            copy.start()
            crosses.append(copy)
        if pair:
            ahead = remote(at(full, j), at(full, j, own), fw_s.at[len(forwards)], fw_r.at[len(forwards)], "kf", former)
            forwards.append(ahead)

            @pl.when(w > 0)
            def _():
                ahead.start()

    def landed(j):
        remote(at(full, j), at(full, j), ag_s.at[0], ag_r.at[j], "lm", partner).wait_recv()

    held = [z] + arrive
    pass_on(i, True)
    for k in range(1, hi + 1):
        if k < hi:
            landed(2 * held[k] + x)
            pass_on(2 * held[k] + x, True)
        landed(2 * held[k - 1] + 1 - x)
        pass_on(2 * held[k - 1] + 1 - x, False)

    def finish_pair():
        @pl.when(w < m - 1)
        def _():
            for copy in forwards:
                copy.wait_recv()

        @pl.when(w == m - 1)
        def _():
            full[pl.ds(own, own)] = jnp.zeros((own,) + full.shape[1:], jnp.float32)

    def finish_sends():
        @pl.when(w < m - 1)
        def _():
            for copy in folds:
                copy.wait_send()

        for copy in twins + scatters + gathers + crosses:
            copy.wait_send()
        if pair:

            @pl.when(w > 0)
            def _():
                for copy in forwards:
                    copy.wait_send()

    return finish_pair, finish_sends


def over_windows(m, value, slots, send, recv):
    w = lax.axis_index("kf")
    slots[w] = jnp.sum(value, axis=0)
    copies = []
    for k in range(1, m):
        copy = remote(slots.at[w], slots.at[w], send.at[k], recv.at[w], "kf", lax.rem(w + k, m))
        copy.start()
        copies.append(copy)
    for k in range(1, m):
        j = lax.rem(w + k, m)
        remote(slots.at[j], slots.at[j], send.at[0], recv.at[j], "kf", j).wait_recv()
    total = slots[0]
    for j in range(1, m):
        total = total + slots[j]

    def finish():
        for copy in copies:
            copy.wait_send()

    return jnp.sum(jnp.sum(total, axis=0, keepdims=True), axis=1, keepdims=True), finish


def columns(g):
    return pl.ds(g * LANES, LANES)


def first_phase(n, m, h, damping, jacobi_scale, res_out, dir_out, energy_out, diag_out, full, fold, acc, twin, rs, slots, diag, *sems):
    own = acc.shape[0]
    state = damping.shape[0]
    w = lax.axis_index("kf")
    diag[...] = jnp.zeros_like(diag)
    for g in range(own):
        diag[g, pl.ds(0, state), :] = damping[:, columns(g)]
        diag[g, pl.ds(PAD, state), :] = jacobi_scale[:, columns(g)]
    greet(n, m)
    diag_copy = remote(
        diag.at[pl.ds(0, own)], diag.at[pl.ds(own, own)], sems[13].at[0], sems[13].at[1], "kf", lax.rem(w + m - 1, m)
    )

    @pl.when(w > 0)
    def _():
        diag_copy.start()

    finish_pair, finish_sends = reduce_spread(n, m, True, h, full, (fold, acc, twin, rs), sems[:11])
    grad = full[pl.ds(0, own)]
    scale = diag[pl.ds(0, own), pl.ds(PAD, PAD), :]
    energy, finish = over_windows(m, grad * grad * scale, slots.at[0], sems[11].at[0], sems[12].at[0])
    energy_out[...] = jnp.broadcast_to(energy, energy_out.shape)
    finish_pair()

    @pl.when(w < m - 1)
    def _():
        diag_copy.wait_recv()

    @pl.when(w > 0)
    def _():
        diag_copy.wait_send()

    res_out[...] = -full[...]
    dir_out[...] = -full[...] * diag[:, pl.ds(PAD, PAD), :]
    diag_out[...] = diag[...]
    finish()
    finish_sends()


def middle_phase(begun, n, m, h, res, direction, diag, energy_in, *rest):
    if begun:
        answer_in, *rest = rest
    res_out, dir_out, energy_out, answer_out, full, fold, acc, twin, rs, slots, *sems = rest
    own = acc.shape[0]
    here, damp, scale = pl.ds(0, own), pl.ds(0, PAD), pl.ds(PAD, PAD)
    greet(n, m)
    finish_pair, finish_sends = reduce_spread(n, m, True, h, full, (fold, acc, twin, rs), sems[:11])
    energy = energy_in[pl.ds(0, 1), pl.ds(0, 1)]
    applied = full[here] + diag[here, damp, :] * direction[here]
    curve, finish_a = over_windows(m, direction[here] * applied, slots.at[0], sems[11].at[0], sems[12].at[0])
    step = energy / curve
    after = res[here] - step * applied
    fresh, finish_b = over_windows(m, after * after * diag[here, scale, :], slots.at[1], sems[11].at[1], sems[12].at[1])
    gained = step * direction[here]
    answer_out[...] = answer_in[...] + gained if begun else gained
    energy_out[...] = jnp.broadcast_to(fresh, energy_out.shape)
    finish_pair()
    after = res[...] - step * (full[...] + diag[:, damp, :] * direction[...])
    res_out[...] = after
    dir_out[...] = diag[:, scale, :] * after + fresh / energy * direction[...]
    finish_a()
    finish_b()
    finish_sends()


def last_phase(n, m, h, res, direction, diag, energy_in, answer_in, res_out, answer_out, full, fold, acc, twin, rs, slots, *sems):
    own = acc.shape[0]
    state = res_out.shape[0]
    here = pl.ds(0, own)
    greet(n, m)
    _, finish_sends = reduce_spread(n, m, False, h, full, (fold, acc, twin, rs), sems[:11])
    applied = full[here] + diag[here, pl.ds(0, PAD), :] * direction[here]
    curve, finish = over_windows(m, direction[here] * applied, slots.at[0], sems[11].at[0], sems[12].at[0])
    step = energy_in[pl.ds(0, 1), pl.ds(0, 1)] / curve
    for g in range(own):
        answer_out[:, columns(g)] = (answer_in[g] + step * direction[g])[:state]
        res_out[:, columns(g)] = (res[g] - step * (full[g] + diag[g, pl.ds(0, PAD), :] * direction[g]))[:state]
    finish()
    finish_sends()


def phase(kernel, name, number, n, m, outs, extra, *operands):
    pair = operands[0].shape
    own = pair[0] // 2
    tile = pair[1:]
    vmem = pl.BlockSpec(memory_space=pltpu.VMEM)
    dma = pltpu.SemaphoreType.DMA
    return pl.pallas_call(
        functools.partial(kernel, n, m),
        in_specs=[vmem] * len(operands),
        out_specs=[vmem] * len(outs),
        out_shape=[jax.ShapeDtypeStruct(shape, jnp.float32) for shape in outs],
        scratch_shapes=[
            pltpu.VMEM(pair, jnp.float32),
            pltpu.VMEM((own,) + tile, jnp.float32),
            pltpu.VMEM((own,) + tile, jnp.float32),
            pltpu.VMEM((n // 2, own // n) + tile, jnp.float32),
            pltpu.VMEM((n // 2, own // n) + tile, jnp.float32),
            pltpu.VMEM((2, m) + tile, jnp.float32),
        ]
        + [pltpu.VMEM(shape, jnp.float32) for shape in extra]
        + [dma((n,))] * 11
        + [dma((2, m))] * 2
        + [dma((2,))],
        compiler_params=pltpu.CompilerParams(collective_id=number, has_side_effects=True),
        name=name,
    )(*operands)


def prepare(frame_ids, obs_count, first_frame, groups):
    rel = frame_ids - first_frame
    starts = jnp.minimum(rel[:, 0] // LANES, groups - SPAN)
    slots = lax.broadcasted_iota(jnp.int32, rel.shape, 1)
    off = jnp.where(slots < obs_count[:, None], rel - starts[:, None] * LANES, -1)
    twice = (
        lax.broadcasted_iota(jnp.int32, (rel.shape[1], 2 * rel.shape[1]), 0)
        == lax.broadcasted_iota(jnp.int32, (rel.shape[1], 2 * rel.shape[1]), 1) // 2
    ).astype(jnp.float32)
    code = jnp.dot(off.astype(jnp.float32), twice, precision=lax.Precision.HIGHEST)
    return starts, jnp.round(code).astype(jnp.int32)


def shards(residual_rows, jacobian, nullspace, frame_ids, obs_count, damping, jacobi_scale):
    state, frames = damping.shape
    own = frames // LANES
    starts, code = prepare(frame_ids, obs_count, lax.axis_index("kf") * frames, 2 * own)
    jac = jnp.pad(jacobian, ((0, 0), (0, PAD - state), (0, 0)))
    n, m = lax.axis_size("lm"), lax.axis_size("kf")
    pair, one, tile = (2 * own, PAD, LANES), (own, PAD, LANES), (8, LANES)
    both = (2 * own, 2 * PAD, LANES)

    def product(field):
        return local_terms(True, starts, field, code, jac, nullspace, 2 * own)

    gradient = local_terms(False, starts, residual_rows, code, jac, nullspace, 2 * own)
    residual, direction, energy, diag = phase(
        first_phase, "first_phase", 0, n, m, (pair, pair, tile, both), (both,), gradient, damping, jacobi_scale
    )
    answer = ()
    for number in range(1, ITERS):
        residual, direction, energy, *answer = phase(
            functools.partial(middle_phase, number > 1), "middle_phase", number, n, m, (pair, pair, tile, one), (),
            product(direction), residual, direction, diag, energy, *answer,
        )
    residual, answer = phase(
        last_phase, "last_phase", ITERS, n, m, (damping.shape, damping.shape), (),
        product(direction), residual, direction, diag, energy, *answer,
    )
    return (answer, residual)


def solution(mesh):
    placed = (
        P(("lm", "kf"), None),
        P(("lm", "kf"), None, None),
        P(("lm", "kf"), None, None),
        P(("lm", "kf"), None),
        P(("lm", "kf")),
        P(None, "kf"),
        P(None, "kf"),
    )
    return jax.shard_map(
        shards,
        mesh=mesh,
        in_specs=placed,
        out_specs=(P(None, "kf"), P(None, "kf")),
        check_vma=False,
    )
```

```python
import functools

import jax
import jax.numpy as jnp
from jax import lax
from jax.experimental import pallas as pl
from jax.experimental.pallas import tpu as pltpu
from jax.sharding import PartitionSpec as P

ITERS = 2
LANES = 128
PAD = 16
SPAN = 5
CHUNK = 32


def local_kernel(use_field, starts, field_ref, code_ref, jac_ref, null_ref, out_ref, hot_ref, row_ref):
    step = pl.program_id(0)

    @pl.when(step == 0)
    def _():
        out_ref[...] = jnp.zeros_like(out_ref)

    lane_iota = lax.broadcasted_iota(jnp.int32, (LANES, LANES), 0)
    codes = [code_ref[pl.ds(i, 1), :] for i in range(CHUNK)]
    begin = [starts[step * CHUNK + i] for i in range(CHUNK)]
    for i in range(CHUNK):
        hot = lane_iota == (codes[i] & (LANES - 1))
        hot_ref[i] = jnp.where(hot, 1.0, 0.0).astype(jnp.bfloat16)
    if use_field:
        for i in range(CHUNK):
            window = field_ref[pl.ds(begin[i], SPAN)].reshape(SPAN * PAD, LANES).astype(jnp.bfloat16)
            spots = jnp.dot(window, hot_ref[i], preferred_element_type=jnp.float32)
            part = codes[i] >> 7
            gathered = jnp.zeros((PAD, LANES), jnp.float32)
            for q in range(SPAN):
                gathered = jnp.where(part == q, spots[q * PAD:(q + 1) * PAD], gathered)
            jac = jac_ref[i].astype(jnp.float32)
            row_ref[pl.ds(i, 1), :] = jnp.sum(jac * gathered, axis=0, keepdims=True)
    else:
        row_ref[...] = jnp.where(code_ref[...] >= 0, field_ref[...].astype(jnp.float32), 0.0)
    inner = []
    for i in range(CHUNK):
        lifted = row_ref[pl.ds(i, 1), :].astype(jnp.bfloat16)
        inner.append(jnp.dot(lifted, null_ref[i], preferred_element_type=jnp.float32).astype(jnp.bfloat16))
    for i in range(CHUNK):
        row_ref[pl.ds(i, 1), :] = lax.dot_general(
            inner[i], null_ref[i], (((1,), (1,)), ((), ())), preferred_element_type=jnp.float32
        )
    back = []
    for i in range(CHUNK):
        part = codes[i] >> 7
        terms = jac_ref[i].astype(jnp.float32) * row_ref[pl.ds(i, 1), :]
        placed = jnp.concatenate(
            [jnp.where(part == q, terms, 0.0) for q in range(SPAN)], axis=0
        ).astype(jnp.bfloat16)
        back.append(lax.dot_general(
            placed, hot_ref[i], (((1,), (1,)), ((), ())), preferred_element_type=jnp.float32
        ).reshape(SPAN, PAD, LANES))
    for i in range(CHUNK):
        out_ref[pl.ds(begin[i], SPAN)] += back[i]


def local_terms(use_field, starts, field, code, jac, null, groups):
    blocks = null.shape[0]
    if use_field:
        source = pl.BlockSpec(field.shape, lambda b, s: (0, 0, 0))
    else:
        source = pl.BlockSpec((CHUNK, LANES), lambda b, s: (b, 0))
    return pl.pallas_call(
        functools.partial(local_kernel, use_field),
        grid_spec=pltpu.PrefetchScalarGridSpec(
            num_scalar_prefetch=1,
            grid=(blocks // CHUNK,),
            in_specs=[
                source,
                pl.BlockSpec((CHUNK, LANES), lambda b, s: (b, 0)),
                pl.BlockSpec((CHUNK, PAD, LANES), lambda b, s: (b, 0, 0)),
                pl.BlockSpec((CHUNK, LANES, LANES), lambda b, s: (b, 0, 0)),
            ],
            out_specs=pl.BlockSpec((groups, PAD, LANES), lambda b, s: (0, 0, 0)),
            scratch_shapes=[
                pltpu.VMEM((CHUNK, LANES, LANES), jnp.bfloat16),
                pltpu.VMEM((CHUNK, LANES), jnp.float32),
            ],
        ),
        out_shape=jax.ShapeDtypeStruct((groups, PAD, LANES), jnp.float32),
        name="local_field" if use_field else "local_gradient",
    )(starts, field, code, jac, null)


def remote(src, dst, send, recv, axis, index):
    return pltpu.make_async_remote_copy(
        src_ref=src, dst_ref=dst, send_sem=send, recv_sem=recv,
        device_id={axis: index}, device_id_type=pl.DeviceIdType.MESH,
    )


def greet(n, m):
    i, w = lax.axis_index("lm"), lax.axis_index("kf")
    barrier = pltpu.get_barrier_semaphore()
    for k in range(1, n):
        pl.semaphore_signal(
            barrier, inc=1, device_id={"lm": lax.rem(i + k, n)}, device_id_type=pl.DeviceIdType.MESH
        )
    for k in range(1, m):
        pl.semaphore_signal(
            barrier, inc=1, device_id={"kf": lax.rem(w + k, m)}, device_id_type=pl.DeviceIdType.MESH
        )
    pl.semaphore_wait(barrier, n - 1 + m - 1)


def reduce_spread(n, m, pair, h, full, bufs, sems):
    fold, acc, rs = bufs
    fold_s, fold_r, rs_s, rs_r, ag_s, ag_r, fw_s, fw_r = sems
    own = acc.shape[0]
    sh = own // n
    i, w = lax.axis_index("lm"), lax.axis_index("kf")
    later, former = lax.rem(w + 1, m), lax.rem(w + m - 1, m)

    def at(ref, j, base=0):
        return ref.at[pl.ds(base + j * sh, sh)]

    order = [lax.rem(i + k, n) for k in range(1, n)] + [i]
    others = order[:-1]
    folds = [remote(at(h, j, own), at(fold, j), fold_s.at[k], fold_r.at[k], "kf", later) for k, j in enumerate(order)]

    @pl.when(w < m - 1)
    def _():
        for copy in folds:
            copy.start()

    scatters = [remote(at(acc, j), rs.at[i], rs_s.at[k], rs_r.at[i], "lm", j) for k, j in enumerate(others)]
    for k, j in enumerate(order):
        spot = pl.ds(j * sh, sh)

        @pl.when(w > 0)
        def _():
            folds[k].wait_recv()
            acc[spot] = h[spot] + fold[spot]

        @pl.when(w == 0)
        def _():
            acc[spot] = h[spot]

        if k < n - 1:
            scatters[k].start()
    total = acc[pl.ds(i * sh, sh)]
    arrive = [lax.rem(i + n - k, n) for k in range(1, n)]
    for j in arrive:
        remote(at(acc, j), rs.at[j], rs_s.at[0], rs_r.at[j], "lm", j).wait_recv()
        total = total + rs[j]
    full[pl.ds(i * sh, sh)] = total
    gathers = [remote(at(full, i), at(full, i), ag_s.at[k], ag_r.at[i], "lm", j) for k, j in enumerate(others)]
    for copy in gathers:
        copy.start()
    forwards = []
    for k, j in enumerate([i] + arrive):
        if k > 0:
            remote(at(full, j), at(full, j), ag_s.at[0], ag_r.at[j], "lm", j).wait_recv()
        if pair:
            copy = remote(at(full, j), at(full, j, own), fw_s.at[k], fw_r.at[k], "kf", former)
            forwards.append(copy)

            @pl.when(w > 0)
            def _():
                copy.start()

    def finish_pair():
        @pl.when(w < m - 1)
        def _():
            for copy in forwards:
                copy.wait_recv()

        @pl.when(w == m - 1)
        def _():
            full[pl.ds(own, own)] = jnp.zeros((own,) + full.shape[1:], jnp.float32)

    def finish_sends():
        @pl.when(w < m - 1)
        def _():
            for copy in folds:
                copy.wait_send()

        for copy in scatters + gathers:
            copy.wait_send()
        if pair:

            @pl.when(w > 0)
            def _():
                for copy in forwards:
                    copy.wait_send()

    return finish_pair, finish_sends


def over_windows(m, value, slots, send, recv):
    w = lax.axis_index("kf")
    slots[w] = jnp.sum(value, axis=0)
    copies = []
    for k in range(1, m):
        copy = remote(slots.at[w], slots.at[w], send.at[k], recv.at[w], "kf", lax.rem(w + k, m))
        copy.start()
        copies.append(copy)
    for k in range(1, m):
        j = lax.rem(w + k, m)
        remote(slots.at[j], slots.at[j], send.at[0], recv.at[j], "kf", j).wait_recv()
    total = slots[0]
    for j in range(1, m):
        total = total + slots[j]

    def finish():
        for copy in copies:
            copy.wait_send()

    return jnp.sum(jnp.sum(total, axis=0, keepdims=True), axis=1, keepdims=True), finish


def columns(g):
    return pl.ds(g * LANES, LANES)


def first_phase(n, m, h, damping, jacobi_scale, res_out, dir_out, energy_out, diag_out, full, fold, acc, rs, slots, diag, *sems):
    own = acc.shape[0]
    state = damping.shape[0]
    w = lax.axis_index("kf")
    diag[...] = jnp.zeros_like(diag)
    for g in range(own):
        diag[g, pl.ds(0, state), :] = damping[:, columns(g)]
        diag[g, pl.ds(PAD, state), :] = jacobi_scale[:, columns(g)]
    greet(n, m)
    diag_copy = remote(
        diag.at[pl.ds(0, own)], diag.at[pl.ds(own, own)], sems[10].at[0], sems[10].at[1], "kf", lax.rem(w + m - 1, m)
    )

    @pl.when(w > 0)
    def _():
        diag_copy.start()

    finish_pair, finish_sends = reduce_spread(n, m, True, h, full, (fold, acc, rs), sems[:8])
    grad = full[pl.ds(0, own)]
    scale = diag[pl.ds(0, own), pl.ds(PAD, PAD), :]
    energy, finish = over_windows(m, grad * grad * scale, slots.at[0], sems[8].at[0], sems[9].at[0])
    energy_out[...] = jnp.broadcast_to(energy, energy_out.shape)
    finish_pair()

    @pl.when(w < m - 1)
    def _():
        diag_copy.wait_recv()

    @pl.when(w > 0)
    def _():
        diag_copy.wait_send()

    res_out[...] = -full[...]
    dir_out[...] = -full[...] * diag[:, pl.ds(PAD, PAD), :]
    diag_out[...] = diag[...]
    finish()
    finish_sends()


def middle_phase(begun, n, m, h, res, direction, diag, energy_in, *rest):
    if begun:
        answer_in, *rest = rest
    res_out, dir_out, energy_out, answer_out, full, fold, acc, rs, slots, *sems = rest
    own = acc.shape[0]
    here, damp, scale = pl.ds(0, own), pl.ds(0, PAD), pl.ds(PAD, PAD)
    greet(n, m)
    finish_pair, finish_sends = reduce_spread(n, m, True, h, full, (fold, acc, rs), sems[:8])
    energy = energy_in[pl.ds(0, 1), pl.ds(0, 1)]
    applied = full[here] + diag[here, damp, :] * direction[here]
    curve, finish_a = over_windows(m, direction[here] * applied, slots.at[0], sems[8].at[0], sems[9].at[0])
    step = energy / curve
    after = res[here] - step * applied
    fresh, finish_b = over_windows(m, after * after * diag[here, scale, :], slots.at[1], sems[8].at[1], sems[9].at[1])
    gained = step * direction[here]
    answer_out[...] = answer_in[...] + gained if begun else gained
    energy_out[...] = jnp.broadcast_to(fresh, energy_out.shape)
    finish_pair()
    after = res[...] - step * (full[...] + diag[:, damp, :] * direction[...])
    res_out[...] = after
    dir_out[...] = diag[:, scale, :] * after + fresh / energy * direction[...]
    finish_a()
    finish_b()
    finish_sends()


def last_phase(n, m, h, res, direction, diag, energy_in, answer_in, res_out, applied_out, answer_out, dir_out, step_out, full, fold, acc, rs, slots, *sems):
    own = acc.shape[0]
    state = res_out.shape[0]
    here = pl.ds(0, own)
    greet(n, m)
    for g in range(own):
        res_out[:, columns(g)] = res[g, pl.ds(0, state), :]
        answer_out[:, columns(g)] = answer_in[g, pl.ds(0, state), :]
        dir_out[:, columns(g)] = direction[g, pl.ds(0, state), :]
    _, finish_sends = reduce_spread(n, m, False, h, full, (fold, acc, rs), sems[:8])
    applied = full[here] + diag[here, pl.ds(0, PAD), :] * direction[here]
    curve, finish = over_windows(m, direction[here] * applied, slots.at[0], sems[8].at[0], sems[9].at[0])
    step = energy_in[pl.ds(0, 1), pl.ds(0, 1)] / curve
    step_out[...] = jnp.broadcast_to(step, step_out.shape)
    for g in range(own):
        applied_out[:, columns(g)] = applied[g, :state]
    finish()
    finish_sends()


def phase(kernel, name, number, n, m, outs, extra, *operands):
    pair = operands[0].shape
    own = pair[0] // 2
    tile = pair[1:]
    vmem = pl.BlockSpec(memory_space=pltpu.VMEM)
    dma = pltpu.SemaphoreType.DMA
    return pl.pallas_call(
        functools.partial(kernel, n, m),
        in_specs=[vmem] * len(operands),
        out_specs=[vmem] * len(outs),
        out_shape=[jax.ShapeDtypeStruct(shape, jnp.float32) for shape in outs],
        scratch_shapes=[
            pltpu.VMEM(pair, jnp.float32),
            pltpu.VMEM((own,) + tile, jnp.float32),
            pltpu.VMEM((own,) + tile, jnp.float32),
            pltpu.VMEM((n, own // n) + tile, jnp.float32),
            pltpu.VMEM((2, m) + tile, jnp.float32),
        ]
        + [pltpu.VMEM(shape, jnp.float32) for shape in extra]
        + [dma((n,))] * 8
        + [dma((2, m))] * 2
        + [dma((2,))],
        compiler_params=pltpu.CompilerParams(collective_id=number, has_side_effects=True),
        name=name,
    )(*operands)


def prepare(frame_ids, obs_count, first_frame, groups):
    rel = frame_ids - first_frame
    starts = jnp.minimum(rel[:, 0] // LANES, groups - SPAN)
    slots = lax.broadcasted_iota(jnp.int32, rel.shape, 1)
    off = jnp.where(slots < obs_count[:, None], rel - starts[:, None] * LANES, -1)
    twice = (
        lax.broadcasted_iota(jnp.int32, (rel.shape[1], 2 * rel.shape[1]), 0)
        == lax.broadcasted_iota(jnp.int32, (rel.shape[1], 2 * rel.shape[1]), 1) // 2
    ).astype(jnp.float32)
    code = jnp.dot(off.astype(jnp.float32), twice, precision=lax.Precision.HIGHEST)
    return starts, jnp.round(code).astype(jnp.int32)


def shards(residual_rows, jacobian, nullspace, frame_ids, obs_count, damping, jacobi_scale):
    state, frames = damping.shape
    own = frames // LANES
    starts, code = prepare(frame_ids, obs_count, lax.axis_index("kf") * frames, 2 * own)
    jac = jnp.pad(jacobian, ((0, 0), (0, PAD - state), (0, 0)))
    n, m = lax.axis_size("lm"), lax.axis_size("kf")
    pair, one, tile = (2 * own, PAD, LANES), (own, PAD, LANES), (8, LANES)
    both = (2 * own, 2 * PAD, LANES)

    def product(field):
        return local_terms(True, starts, field, code, jac, nullspace, 2 * own)

    gradient = local_terms(False, starts, residual_rows, code, jac, nullspace, 2 * own)
    residual, direction, energy, diag = phase(
        first_phase, "first_phase", 0, n, m, (pair, pair, tile, both), (both,), gradient, damping, jacobi_scale
    )
    answer = ()
    for number in range(1, ITERS):
        residual, direction, energy, *answer = phase(
            functools.partial(middle_phase, number > 1), "middle_phase", number, n, m, (pair, pair, tile, one), (),
            product(direction), residual, direction, diag, energy, *answer,
        )
    residual, applied, answer, direction, step = phase(
        last_phase, "last_phase", ITERS, n, m, (damping.shape,) * 4 + (tile,), (),
        product(direction), residual, direction, diag, energy, *answer,
    )
    step = step[0, 0]
    return (answer + step * direction, residual - step * applied)


def solution(mesh):
    placed = (
        P(("lm", "kf"), None),
        P(("lm", "kf"), None, None),
        P(("lm", "kf"), None, None),
        P(("lm", "kf"), None),
        P(("lm", "kf")),
        P(None, "kf"),
        P(None, "kf"),
    )
    return jax.shard_map(
        shards,
        mesh=mesh,
        in_specs=placed,
        out_specs=(P(None, "kf"), P(None, "kf")),
        check_vma=False,
    )
```

```python
import functools

import jax
import jax.numpy as jnp
from jax import lax
from jax.experimental import pallas as pl
from jax.experimental.pallas import tpu as pltpu
from jax.sharding import PartitionSpec as P

ITERS = 2
LANES = 128
PAD = 16
SPAN = 5
CHUNK = 32


def local_kernel(use_field, starts, field_ref, code_ref, jac_ref, null_ref, out_ref, hot_ref, row_ref):
    step = pl.program_id(0)

    @pl.when(step == 0)
    def _():
        out_ref[...] = jnp.zeros_like(out_ref)

    lane_iota = lax.broadcasted_iota(jnp.int32, (LANES, LANES), 0)
    codes = [code_ref[pl.ds(i, 1), :] for i in range(CHUNK)]
    begin = [starts[step * CHUNK + i] for i in range(CHUNK)]
    for i in range(CHUNK):
        hot = lane_iota == (codes[i] & (LANES - 1))
        hot_ref[i] = jnp.where(hot, 1.0, 0.0).astype(jnp.bfloat16)
    if use_field:
        for i in range(CHUNK):
            window = field_ref[pl.ds(begin[i], SPAN)].reshape(SPAN * PAD, LANES).astype(jnp.bfloat16)
            spots = jnp.dot(window, hot_ref[i], preferred_element_type=jnp.float32)
            part = codes[i] >> 7
            gathered = jnp.zeros((PAD, LANES), jnp.float32)
            for q in range(SPAN):
                gathered = jnp.where(part == q, spots[q * PAD:(q + 1) * PAD], gathered)
            jac = jac_ref[i].astype(jnp.float32)
            row_ref[pl.ds(i, 1), :] = jnp.sum(jac * gathered, axis=0, keepdims=True)
    else:
        row_ref[...] = jnp.where(code_ref[...] >= 0, field_ref[...].astype(jnp.float32), 0.0)
    inner = []
    for i in range(CHUNK):
        lifted = row_ref[pl.ds(i, 1), :].astype(jnp.bfloat16)
        inner.append(jnp.dot(lifted, null_ref[i], preferred_element_type=jnp.float32).astype(jnp.bfloat16))
    for i in range(CHUNK):
        row_ref[pl.ds(i, 1), :] = lax.dot_general(
            inner[i], null_ref[i], (((1,), (1,)), ((), ())), preferred_element_type=jnp.float32
        )
    back = []
    for i in range(CHUNK):
        part = codes[i] >> 7
        terms = jac_ref[i].astype(jnp.float32) * row_ref[pl.ds(i, 1), :]
        placed = jnp.concatenate(
            [jnp.where(part == q, terms, 0.0) for q in range(SPAN)], axis=0
        ).astype(jnp.bfloat16)
        back.append(lax.dot_general(
            placed, hot_ref[i], (((1,), (1,)), ((), ())), preferred_element_type=jnp.float32
        ).reshape(SPAN, PAD, LANES))
    for i in range(CHUNK):
        out_ref[pl.ds(begin[i], SPAN)] += back[i]


def local_terms(use_field, starts, field, code, jac, null, groups):
    blocks = null.shape[0]
    if use_field:
        source = pl.BlockSpec(field.shape, lambda b, s: (0, 0, 0))
    else:
        source = pl.BlockSpec((CHUNK, LANES), lambda b, s: (b, 0))
    return pl.pallas_call(
        functools.partial(local_kernel, use_field),
        grid_spec=pltpu.PrefetchScalarGridSpec(
            num_scalar_prefetch=1,
            grid=(blocks // CHUNK,),
            in_specs=[
                source,
                pl.BlockSpec((CHUNK, LANES), lambda b, s: (b, 0)),
                pl.BlockSpec((CHUNK, PAD, LANES), lambda b, s: (b, 0, 0)),
                pl.BlockSpec((CHUNK, LANES, LANES), lambda b, s: (b, 0, 0)),
            ],
            out_specs=pl.BlockSpec((groups, PAD, LANES), lambda b, s: (0, 0, 0)),
            scratch_shapes=[
                pltpu.VMEM((CHUNK, LANES, LANES), jnp.bfloat16),
                pltpu.VMEM((CHUNK, LANES), jnp.float32),
            ],
        ),
        out_shape=jax.ShapeDtypeStruct((groups, PAD, LANES), jnp.float32),
        name="local_field" if use_field else "local_gradient",
    )(starts, field, code, jac, null)


def remote(src, dst, send, recv, axis, index):
    return pltpu.make_async_remote_copy(
        src_ref=src, dst_ref=dst, send_sem=send, recv_sem=recv,
        device_id={axis: index}, device_id_type=pl.DeviceIdType.MESH,
    )


def greet(n, m):
    i, w = lax.axis_index("lm"), lax.axis_index("kf")
    barrier = pltpu.get_barrier_semaphore()
    for k in range(1, n):
        pl.semaphore_signal(
            barrier, inc=1, device_id={"lm": lax.rem(i + k, n)}, device_id_type=pl.DeviceIdType.MESH
        )
    for k in range(1, m):
        pl.semaphore_signal(
            barrier, inc=1, device_id={"kf": lax.rem(w + k, m)}, device_id_type=pl.DeviceIdType.MESH
        )
    pl.semaphore_wait(barrier, n - 1 + m - 1)


def reduce_spread(n, m, pair, h, full, bufs, sems):
    fold, acc, rs = bufs
    fold_s, fold_r, rs_s, rs_r, ag_s, ag_r, fw_s, fw_r = sems
    own = acc.shape[0]
    sh = own // n
    i, w = lax.axis_index("lm"), lax.axis_index("kf")
    later, former = lax.rem(w + 1, m), lax.rem(w + m - 1, m)

    def at(ref, j, base=0):
        return ref.at[pl.ds(base + j * sh, sh)]

    order = [lax.rem(i + k, n) for k in range(1, n)] + [i]
    others = order[:-1]
    folds = [remote(at(h, j, own), at(fold, j), fold_s.at[k], fold_r.at[k], "kf", later) for k, j in enumerate(order)]

    @pl.when(w < m - 1)
    def _():
        for copy in folds:
            copy.start()

    scatters = [remote(at(acc, j), rs.at[i], rs_s.at[k], rs_r.at[i], "lm", j) for k, j in enumerate(others)]
    for k, j in enumerate(order):
        spot = pl.ds(j * sh, sh)

        @pl.when(w > 0)
        def _():
            folds[k].wait_recv()
            acc[spot] = h[spot] + fold[spot]

        @pl.when(w == 0)
        def _():
            acc[spot] = h[spot]

        if k < n - 1:
            scatters[k].start()
    total = acc[pl.ds(i * sh, sh)]
    arrive = [lax.rem(i + n - k, n) for k in range(1, n)]
    for j in arrive:
        remote(at(acc, j), rs.at[j], rs_s.at[0], rs_r.at[j], "lm", j).wait_recv()
        total = total + rs[j]
    full[pl.ds(i * sh, sh)] = total
    gathers = [remote(at(full, i), at(full, i), ag_s.at[k], ag_r.at[i], "lm", j) for k, j in enumerate(others)]
    for copy in gathers:
        copy.start()
    forwards = []
    for k, j in enumerate([i] + arrive):
        if k > 0:
            remote(at(full, j), at(full, j), ag_s.at[0], ag_r.at[j], "lm", j).wait_recv()
        if pair:
            copy = remote(at(full, j), at(full, j, own), fw_s.at[k], fw_r.at[k], "kf", former)
            forwards.append(copy)

            @pl.when(w > 0)
            def _():
                copy.start()

    def finish_pair():
        @pl.when(w < m - 1)
        def _():
            for copy in forwards:
                copy.wait_recv()

        @pl.when(w == m - 1)
        def _():
            full[pl.ds(own, own)] = jnp.zeros((own,) + full.shape[1:], jnp.float32)

    def finish_sends():
        @pl.when(w < m - 1)
        def _():
            for copy in folds:
                copy.wait_send()

        for copy in scatters + gathers:
            copy.wait_send()
        if pair:

            @pl.when(w > 0)
            def _():
                for copy in forwards:
                    copy.wait_send()

    return finish_pair, finish_sends


def over_windows(m, value, slots, send, recv):
    w = lax.axis_index("kf")
    slots[w] = jnp.sum(value, axis=0)
    copies = []
    for k in range(1, m):
        copy = remote(slots.at[w], slots.at[w], send.at[k], recv.at[w], "kf", lax.rem(w + k, m))
        copy.start()
        copies.append(copy)
    for k in range(1, m):
        j = lax.rem(w + k, m)
        remote(slots.at[j], slots.at[j], send.at[0], recv.at[j], "kf", j).wait_recv()
    total = slots[0]
    for j in range(1, m):
        total = total + slots[j]

    def finish():
        for copy in copies:
            copy.wait_send()

    return jnp.sum(jnp.sum(total, axis=0, keepdims=True), axis=1, keepdims=True), finish


def columns(g):
    return pl.ds(g * LANES, LANES)


def first_phase(n, m, h, damping, jacobi_scale, res_out, dir_out, energy_out, diag_out, full, fold, acc, rs, slots, diag, *sems):
    own = acc.shape[0]
    state = damping.shape[0]
    w = lax.axis_index("kf")
    diag[...] = jnp.zeros_like(diag)
    for g in range(own):
        diag[g, pl.ds(0, state), :] = damping[:, columns(g)]
        diag[g, pl.ds(PAD, state), :] = jacobi_scale[:, columns(g)]
    greet(n, m)
    diag_copy = remote(
        diag.at[pl.ds(0, own)], diag.at[pl.ds(own, own)], sems[10].at[0], sems[10].at[1], "kf", lax.rem(w + m - 1, m)
    )

    @pl.when(w > 0)
    def _():
        diag_copy.start()

    finish_pair, finish_sends = reduce_spread(n, m, True, h, full, (fold, acc, rs), sems[:8])
    grad = full[pl.ds(0, own)]
    scale = diag[pl.ds(0, own), pl.ds(PAD, PAD), :]
    energy, finish = over_windows(m, grad * grad * scale, slots.at[0], sems[8].at[0], sems[9].at[0])
    energy_out[...] = jnp.broadcast_to(energy, energy_out.shape)
    finish_pair()

    @pl.when(w < m - 1)
    def _():
        diag_copy.wait_recv()

    @pl.when(w > 0)
    def _():
        diag_copy.wait_send()

    res_out[...] = -full[...]
    dir_out[...] = -full[...] * diag[:, pl.ds(PAD, PAD), :]
    diag_out[...] = diag[...]
    finish()
    finish_sends()


def middle_phase(begun, n, m, h, res, direction, diag, energy_in, *rest):
    if begun:
        answer_in, *rest = rest
    res_out, dir_out, energy_out, answer_out, full, fold, acc, rs, slots, *sems = rest
    own = acc.shape[0]
    here, damp, scale = pl.ds(0, own), pl.ds(0, PAD), pl.ds(PAD, PAD)
    greet(n, m)
    finish_pair, finish_sends = reduce_spread(n, m, True, h, full, (fold, acc, rs), sems[:8])
    energy = energy_in[pl.ds(0, 1), pl.ds(0, 1)]
    applied = full[here] + diag[here, damp, :] * direction[here]
    curve, finish_a = over_windows(m, direction[here] * applied, slots.at[0], sems[8].at[0], sems[9].at[0])
    step = energy / curve
    after = res[here] - step * applied
    fresh, finish_b = over_windows(m, after * after * diag[here, scale, :], slots.at[1], sems[8].at[1], sems[9].at[1])
    gained = step * direction[here]
    answer_out[...] = answer_in[...] + gained if begun else gained
    energy_out[...] = jnp.broadcast_to(fresh, energy_out.shape)
    finish_pair()
    after = res[...] - step * (full[...] + diag[:, damp, :] * direction[...])
    res_out[...] = after
    dir_out[...] = diag[:, scale, :] * after + fresh / energy * direction[...]
    finish_a()
    finish_b()
    finish_sends()


def last_phase(n, m, h, direction, diag, energy_in, applied_out, step_out, full, fold, acc, rs, slots, *sems):
    own = acc.shape[0]
    here = pl.ds(0, own)
    greet(n, m)
    _, finish_sends = reduce_spread(n, m, False, h, full, (fold, acc, rs), sems[:8])
    applied = full[here] + diag[here, pl.ds(0, PAD), :] * direction[here]
    applied_out[...] = applied
    curve, finish = over_windows(m, direction[here] * applied, slots.at[0], sems[8].at[0], sems[9].at[0])
    step = energy_in[pl.ds(0, 1), pl.ds(0, 1)] / curve
    step_out[...] = jnp.broadcast_to(step, step_out.shape)
    finish()
    finish_sends()


def update_kernel(res, direction, applied, answer_in, step_in, answer_out, res_out):
    own = applied.shape[0]
    state = res_out.shape[0]
    step = step_in[pl.ds(0, 1), pl.ds(0, 1)]
    for g in range(own):
        answer_out[:, columns(g)] = (answer_in[g] + step * direction[g])[:state]
        res_out[:, columns(g)] = (res[g] - step * applied[g])[:state]


def last_update(shape, res, direction, applied, answer, step):
    half = pl.BlockSpec(applied.shape, lambda i: (0, 0, 0))
    whole = pl.BlockSpec(shape, lambda i: (0, 0))
    return pl.pallas_call(
        update_kernel,
        grid=(1,),
        in_specs=[half] * 4 + [pl.BlockSpec(step.shape, lambda i: (0, 0))],
        out_specs=[whole] * 2,
        out_shape=[jax.ShapeDtypeStruct(shape, jnp.float32)] * 2,
        name="last_update",
    )(res, direction, applied, answer, step)


def phase(kernel, name, number, n, m, outs, extra, *operands):
    pair = operands[0].shape
    own = pair[0] // 2
    tile = pair[1:]
    vmem = pl.BlockSpec(memory_space=pltpu.VMEM)
    dma = pltpu.SemaphoreType.DMA
    return pl.pallas_call(
        functools.partial(kernel, n, m),
        in_specs=[vmem] * len(operands),
        out_specs=[vmem] * len(outs),
        out_shape=[jax.ShapeDtypeStruct(shape, jnp.float32) for shape in outs],
        scratch_shapes=[
            pltpu.VMEM(pair, jnp.float32),
            pltpu.VMEM((own,) + tile, jnp.float32),
            pltpu.VMEM((own,) + tile, jnp.float32),
            pltpu.VMEM((n, own // n) + tile, jnp.float32),
            pltpu.VMEM((2, m) + tile, jnp.float32),
        ]
        + [pltpu.VMEM(shape, jnp.float32) for shape in extra]
        + [dma((n,))] * 8
        + [dma((2, m))] * 2
        + [dma((2,))],
        compiler_params=pltpu.CompilerParams(collective_id=number, has_side_effects=True),
        name=name,
    )(*operands)


def prepare(frame_ids, obs_count, first_frame, groups):
    rel = frame_ids - first_frame
    starts = jnp.minimum(rel[:, 0] // LANES, groups - SPAN)
    slots = lax.broadcasted_iota(jnp.int32, rel.shape, 1)
    off = jnp.where(slots < obs_count[:, None], rel - starts[:, None] * LANES, -1)
    twice = (
        lax.broadcasted_iota(jnp.int32, (rel.shape[1], 2 * rel.shape[1]), 0)
        == lax.broadcasted_iota(jnp.int32, (rel.shape[1], 2 * rel.shape[1]), 1) // 2
    ).astype(jnp.float32)
    code = jnp.dot(off.astype(jnp.float32), twice, precision=lax.Precision.HIGHEST)
    return starts, jnp.round(code).astype(jnp.int32)


def shards(residual_rows, jacobian, nullspace, frame_ids, obs_count, damping, jacobi_scale):
    state, frames = damping.shape
    own = frames // LANES
    starts, code = prepare(frame_ids, obs_count, lax.axis_index("kf") * frames, 2 * own)
    jac = jnp.pad(jacobian, ((0, 0), (0, PAD - state), (0, 0)))
    n, m = lax.axis_size("lm"), lax.axis_size("kf")
    pair, one, tile = (2 * own, PAD, LANES), (own, PAD, LANES), (8, LANES)
    both = (2 * own, 2 * PAD, LANES)

    def product(field):
        return local_terms(True, starts, field, code, jac, nullspace, 2 * own)

    gradient = local_terms(False, starts, residual_rows, code, jac, nullspace, 2 * own)
    residual, direction, energy, diag = phase(
        first_phase, "first_phase", 0, n, m, (pair, pair, tile, both), (both,), gradient, damping, jacobi_scale
    )
    answer = ()
    for number in range(1, ITERS):
        residual, direction, energy, *answer = phase(
            functools.partial(middle_phase, number > 1), "middle_phase", number, n, m, (pair, pair, tile, one), (),
            product(direction), residual, direction, diag, energy, *answer,
        )
    applied, step = phase(
        last_phase, "last_phase", ITERS, n, m, (one, tile), (), product(direction), direction, diag, energy
    )
    return tuple(last_update(damping.shape, residual, direction, applied, *answer, step))


def solution(mesh):
    placed = (
        P(("lm", "kf"), None),
        P(("lm", "kf"), None, None),
        P(("lm", "kf"), None, None),
        P(("lm", "kf"), None),
        P(("lm", "kf")),
        P(None, "kf"),
        P(None, "kf"),
    )
    return jax.shard_map(
        shards,
        mesh=mesh,
        in_specs=placed,
        out_specs=(P(None, "kf"), P(None, "kf")),
        check_vma=False,
    )
```
